1024 devices in a mesh: dp: 64 (over x_hi, z, core), group: 16 (over x_lo, y).
Axes of the slice: x: 8 (x_hi: 4, x_lo: 2; x = x_hi * 2 + x_lo), y: 8, z: 8, core: 2. Of those that a mesh axis runs over, the one named last changes fastest.
Arguments:
- layer_input: bfloat16 [16384, 8192], P('dp', 'group'), may hold values from -30 to 30
- kv_cotangent: bfloat16 [16384, 2048], P('dp', 'group'), may hold values from -70 to 70
- weight_codes: bfloat16 [2048, 8192], P('dp', 'group'), may hold values from -256 to 256
- block_scales: bfloat16 [2048, 32], P('dp', 'group'), may hold values from 0.00024986267 to 0.0009994507
- master: float32 [2048, 8192], P('dp', 'group'), may hold values from -6 to 6
- moment_one: float32 [2048, 8192], P('dp', 'group'), may hold values from -0.75 to 0.75
- moment_two: float32 [2048, 8192], P('dp', 'group'), may hold values from 0.001 to 0.01
Outputs:
- grad_input: bfloat16 [16384, 8192], P('dp', 'group')
- new_master: float32 [2048, 8192], P('dp', 'group')
- new_moment_one: float32 [2048, 8192], P('dp', 'group')
- new_moment_two: float32 [2048, 8192], P('dp', 'group')
The draws below stay inside these ranges and needn't reach their ends.
All inputs are finite; a program needn't handle non-finite values.
Results may differ from the reference program's by a relative error of at most 0.0049.
Values may be sent and summed in bfloat16 or wider, within the bound.
No kernel may reach another device: no remote copies, remote signals or barrier semaphores. Data moves between devices by JAX's collectives and lax.ppermute only.
A program may use at most 32 MiB of HBM per device.

```python
import math
import jax
import jax.numpy as jnp
from jax import lax

D = 8192
BLOCK = 256
CLIP = 2048
TOK_DEV = 256
KV_COLS = 2048
TOKENS = 16384
N_DP = 64


def column_scales(key, number, rise):
    spread = jax.random.uniform(key, (number,), jnp.float32)
    trend = jnp.arange(number, dtype=jnp.float32) / number
    return jnp.exp(2.302585 * spread + rise * trend) / 4.0


def token_signs(base_key):
    flips = jax.random.randint(jax.random.fold_in(base_key, 41), (TOKENS,), 0, 2)
    return 2.0 * flips.astype(jnp.float32) - 1.0


def scaled_field(key, signs, rows_total, cols_total):
    first_key, second_key, third_key = jax.random.split(key, 3)
    common = jnp.clip(jax.random.normal(third_key, (cols_total,), jnp.float32), -2.0, 2.0)
    shared_weight = float(TOKENS) ** (-0.25)
    values = jnp.clip(jax.random.normal(first_key, (rows_total, cols_total), jnp.float32), -4.0, 4.0)
    scales = column_scales(second_key, cols_total, 0.55)
    values = values + shared_weight * signs[:, None] * common[None, :]
    return values * scales[None, :]


def draw_layer_input(key, part):
    signs = token_signs(key)
    field = scaled_field(jax.random.fold_in(key, 17), signs, TOKENS, D)
    return jnp.clip(field, -30.0, 30.0).astype(jnp.bfloat16)


def draw_kv_cotangent(key, part):
    signs = token_signs(key)
    field_key, pair_key = jax.random.split(jax.random.fold_in(key, 29), 2)
    values = scaled_field(field_key, signs, TOKENS, KV_COLS)
    pairing = jax.random.permutation(pair_key, N_DP)
    row_block = jnp.arange(TOKENS) // TOK_DEV
    col_block = jnp.arange(KV_COLS) // (KV_COLS // N_DP)
    boost = jnp.where(pairing[row_block][:, None] == col_block[None, :], 3.0, 1.0)
    return jnp.clip(values * boost, -70.0, 70.0).astype(jnp.bfloat16)


def steps_of(own_key, shape, cuts, low, top_value):
    loudness, own = 1.0, jax.random.fold_in(own_key, 6)
    for position, parts in cuts:
        heights = jnp.exp(jax.random.uniform(jax.random.fold_in(own, position), (parts,), jnp.float32, low / len(cuts), top_value / len(cuts)))
        loudness = loudness * jnp.repeat(heights, shape[position] // parts).reshape([-1 if axis == position else 1 for axis in range(len(shape))])
    return loudness


def bell_draw(stream_key, shape, scale, reach, pieces=(), kind=jnp.bfloat16):
    level = steps_of(stream_key, shape, pieces, -0.22, 0.18) if pieces else 1.0
    array = jax.random.normal(stream_key, shape, jnp.float32) * scale * level
    return jnp.minimum(jnp.maximum(array, -reach), reach).astype(kind)


def setup_inputs(seed: int = 0) -> dict:
    streams_of = jax.random.split(jax.random.key(seed), 8)
    return {
        "layer_input": draw_layer_input(jax.random.fold_in(streams_of[7], 71), 0),
        "kv_cotangent": draw_kv_cotangent(jax.random.fold_in(streams_of[7], 71), 0),
        "weight_codes": bell_draw(streams_of[2], (KV_COLS, D), 40.0, 256.0, ((0, 64), (1, 16))),
        "block_scales": jnp.clip(jnp.exp(math.log(0.0009994507) - 1.3862944 * jax.random.uniform(streams_of[3], (KV_COLS, D // BLOCK), jnp.float32) ** steps_of(streams_of[3], (KV_COLS, D // BLOCK), ((0, 64), (1, 16)), -0.2, 0.2)), 0.00024986267, 0.0009994507).astype(jnp.bfloat16),
        "master": bell_draw(streams_of[4], (KV_COLS, D), 0.5, 6.0, ((0, 64), (1, 16)), jnp.float32),
        "moment_one": bell_draw(streams_of[5], (KV_COLS, D), 0.05, 0.75, ((0, 64), (1, 16)), jnp.float32),
        "moment_two": jnp.clip(jnp.exp(math.log(0.01) - 2.30258502 * jax.random.uniform(streams_of[6], (KV_COLS, D), jnp.float32) ** steps_of(streams_of[6], (KV_COLS, D), ((0, 64), (1, 16)), -0.2, 0.2)), 0.001, 0.01),
    }


BETA_ONE = 0.9
BETA_TWO = 0.95
LEARN_RATE = 0.25
DECAY_RATE = 0.1
EPS_ADAM = 1e-08
EPS_NORM = 1e-06

def reference(layer_input, kv_cotangent, weight_codes, block_scales, master, moment_one, moment_two):
    blocked = weight_codes.astype(jnp.float32).reshape(KV_COLS, D // BLOCK, BLOCK) * block_scales.astype(jnp.float32)[:, :, None]
    weight = blocked.reshape(KV_COLS, D).astype(jnp.bfloat16)
    grad_input = jnp.dot(kv_cotangent, weight, preferred_element_type=jnp.float32).astype(jnp.bfloat16)
    input_runs = layer_input.reshape(N_DP, TOK_DEV, D)
    cot_runs = kv_cotangent.reshape(N_DP, TOK_DEV, KV_COLS)

    def accumulate(running, pair):
        partial_value = jnp.dot(pair[1].T, pair[0], preferred_element_type=jnp.float32)
        rounded = lax.optimization_barrier(partial_value.astype(jnp.bfloat16))
        return (running + rounded.astype(jnp.float32), None)
    gradient, _ = lax.scan(accumulate, jnp.zeros((KV_COLS, D), jnp.float32), (input_runs, cot_runs))
    norm_value = jnp.sqrt(jnp.sum(gradient * gradient))
    factor = jnp.minimum(1.0, CLIP / (norm_value + EPS_NORM))
    clipped = gradient * factor
    new_moment_one = BETA_ONE * moment_one + (1.0 - BETA_ONE) * clipped
    new_moment_two = BETA_TWO * moment_two + (1.0 - BETA_TWO) * clipped * clipped
    first_fix = 1.0 - BETA_ONE ** 10
    second_fix = 1.0 - BETA_TWO ** 10
    update = new_moment_one / first_fix / (jnp.sqrt(new_moment_two / second_fix) + EPS_ADAM)
    new_master = master - LEARN_RATE * (update + DECAY_RATE * master)
    return (grad_input, new_master, new_moment_one, new_moment_two)
```

```python
import jax
import jax.numpy as jnp
from jax import lax
from jax.sharding import Mesh
from jax.sharding import PartitionSpec as P

BLOCK = 256
CLIP = 2048


BETA_ONE = 0.9
BETA_TWO = 0.95
LEARN_RATE = 0.25
DECAY_RATE = 0.1
EPS_ADAM = 1e-08
EPS_NORM = 1e-06

SIZES = {"xh": 4, "z": 8, "core": 2, "xl": 2, "y": 8}
DP = ("xh", "z", "core")
GROUP = ("xl", "y")
CHIPS = ("xh", "z")
N_CHIPS = 32
N_GROUP = 16


def dequantize(codes, scales):
    row_count, col_count = codes.shape
    blocked = (
        codes.astype(jnp.float32).reshape(row_count, col_count // BLOCK, BLOCK)
        * scales.astype(jnp.float32)[:, :, None]
    )
    return blocked.reshape(row_count, col_count).astype(jnp.bfloat16)


def spread(block, axes, count):
    return lax.all_to_all(jnp.broadcast_to(block[None], (count, *block.shape)), axes, 0, 0)


def swap_cores(block):
    return lax.ppermute(block, "core", [(0, 1), (1, 0)])


def total(value, axes, count):
    return jnp.sum(spread(value, axes, count), axis=0)


def shards(layer_input, kv_cotangent, weight_codes, block_scales, master, moment_one, moment_two):
    core = lax.axis_index("core")
    rows, cols = weight_codes.shape

    weight_mine = spread(dequantize(weight_codes, block_scales), CHIPS, N_CHIPS)
    weight_other = swap_cores(weight_mine)
    weight = jnp.where(
        core == 0,
        jnp.stack([weight_mine, weight_other], axis=1),
        jnp.stack([weight_other, weight_mine], axis=1),
    ).reshape(N_CHIPS * 2 * rows, cols)

    cot = spread(kv_cotangent, GROUP, N_GROUP)
    cot_whole = cot.transpose(1, 0, 2).reshape(kv_cotangent.shape[0], -1)
    partial_value = jnp.einsum(
        "tc,td->cd", cot_whole, layer_input, preferred_element_type=jnp.float32
    ).astype(jnp.bfloat16)
    halves = partial_value.reshape(N_CHIPS, 2, rows, cols)
    keep = lax.dynamic_index_in_dim(halves, core, 1, keepdims=False)
    give = lax.dynamic_index_in_dim(halves, 1 - core, 1, keepdims=False)
    pair = keep.astype(jnp.float32) + swap_cores(give).astype(jnp.float32)
    pieces = lax.all_to_all(pair.astype(jnp.bfloat16), CHIPS, 0, 0)
    gradient = jnp.sum(pieces.astype(jnp.float32), axis=0)

    squares = jnp.sum((gradient * gradient).reshape(-1, 8, 128), axis=0)
    square_total = jnp.sum(total(total(squares, DP, 64), GROUP, N_GROUP))
    factor = jnp.minimum(1.0, CLIP / (jnp.sqrt(square_total) + EPS_NORM))
    clipped = gradient * factor
    new_moment_one = BETA_ONE * moment_one + (1.0 - BETA_ONE) * clipped
    new_moment_two = BETA_TWO * moment_two + (1.0 - BETA_TWO) * clipped * clipped
    first_fix = 1.0 - BETA_ONE**10
    second_fix = 1.0 - BETA_TWO**10
    update = new_moment_one / first_fix / (jnp.sqrt(new_moment_two / second_fix) + EPS_ADAM)
    new_master = master - LEARN_RATE * (update + DECAY_RATE * master)

    grad_input = jnp.dot(cot_whole, weight, preferred_element_type=jnp.float32).astype(jnp.bfloat16)
    return (grad_input, new_master, new_moment_one, new_moment_two)


def solution(mesh):
    fine = Mesh(mesh.devices.reshape(tuple(SIZES.values())), tuple(SIZES))
    return jax.shard_map(
        shards,
        mesh=fine,
        in_specs=(P(DP, GROUP),) * 7,
        out_specs=(P(DP, GROUP),) * 4,
        check_vma=False,
    )
```

```python
import functools

import jax
import jax.numpy as jnp
from jax import lax
from jax.experimental import pallas as pl
from jax.experimental.pallas import tpu as pltpu
from jax.sharding import Mesh
from jax.sharding import PartitionSpec as P

BLOCK = 256
CLIP = 2048


BETA_ONE = 0.9
BETA_TWO = 0.95
LEARN_RATE = 0.25
DECAY_RATE = 0.1
EPS_ADAM = 1e-08
EPS_NORM = 1e-06

SIZES = {"xh": 4, "z": 8, "core": 2, "xl": 2, "y": 8}
DP = ("xh", "z", "core")
GROUP = ("xl", "y")
CHIPS = ("xh", "z")
N_CHIPS = 32
N_GROUP = 16
N_ALL = 1024


def dequantize(codes, scales):
    row_count, col_count = codes.shape
    blocked = (
        codes.astype(jnp.float32).reshape(row_count, col_count // BLOCK, BLOCK)
        * scales.astype(jnp.float32)[:, :, None]
    )
    return blocked.reshape(row_count, col_count).astype(jnp.bfloat16)


def spread(block, axes, count):
    return lax.all_to_all(jnp.broadcast_to(block[None], (count, *block.shape)), axes, 0, 0)


def swap_cores(block):
    return lax.ppermute(block, "core", [(0, 1), (1, 0)])


def fetch(block, axis, distance):
    size = SIZES[axis]
    return lax.ppermute(block, axis, [(i, (i - distance) % size) for i in range(size)])


def collect(block, order, axis, distances):
    for d in distances:
        block = jnp.concatenate([block, fetch(block, axis, d)], axis=0)
        order = order + [(x + d, z) if axis == "xh" else (x, z + d) for x, z in order]
    return block, order


def order_rows_kernel(order, rows, place_ref, mine_ref, other_ref, out_ref):
    x_own, z_own, core = place_ref[0], place_ref[1], place_ref[2]
    for i, (dx, dz) in enumerate(order):
        chip = lax.rem(x_own + dx, SIZES["xh"]) * SIZES["z"] + lax.rem(z_own + dz, SIZES["z"])
        for source, side in ((mine_ref, core), (other_ref, 1 - core)):
            start = pl.multiple_of((chip * 2 + side) * rows, rows)
            out_ref[pl.ds(start, rows), :] = source[i * rows : (i + 1) * rows, :]


def order_rows(mine, other, order, rows):
    place = jnp.stack([lax.axis_index("xh"), lax.axis_index("z"), lax.axis_index("core")])
    size = 2 * mine.shape[0] * mine.shape[1]
    return pl.pallas_call(
        functools.partial(order_rows_kernel, order, rows),
        out_shape=jax.ShapeDtypeStruct((2 * mine.shape[0], mine.shape[1]), mine.dtype),
        in_specs=[
            pl.BlockSpec(memory_space=pltpu.SMEM),
            pl.BlockSpec(memory_space=pltpu.VMEM),
            pl.BlockSpec(memory_space=pltpu.VMEM),
        ],
        out_specs=pl.BlockSpec(memory_space=pltpu.VMEM),
        cost_estimate=pl.CostEstimate(flops=0, bytes_accessed=4 * size, transcendentals=0),
        compiler_params=pltpu.CompilerParams(vmem_limit_bytes=8 * 2**20),
        name="order_rows",
    )(place.astype(jnp.int32), mine, other)


def shards(layer_input, kv_cotangent, weight_codes, block_scales, master, moment_one, moment_two):
    core = lax.axis_index("core")
    rows, cols = weight_codes.shape
    tokens = kv_cotangent.shape[0]

    cot = spread(kv_cotangent.T, GROUP, N_GROUP).reshape(-1, tokens)
    input_other = swap_cores(layer_input)
    mine, order = collect(dequantize(weight_codes, block_scales), [(0, 0)], "xh", (2, 1))
    mine, order = collect(mine, order, "z", (4,))
    cot, input_other, mine = lax.optimization_barrier((cot, input_other, mine))
    halves = cot.reshape(N_CHIPS, 2, rows, tokens)
    keep = lax.dynamic_index_in_dim(halves, core, 1, keepdims=False)
    cot_other = swap_cores(lax.dynamic_index_in_dim(halves, 1 - core, 1, keepdims=False))
    pair = jnp.einsum("crt,td->crd", keep, layer_input, preferred_element_type=jnp.float32)
    pair += jnp.einsum("crt,td->crd", cot_other, input_other, preferred_element_type=jnp.float32)
    pieces = lax.all_to_all(pair.astype(jnp.bfloat16), CHIPS, 0, 0)
    mine, order = collect(mine, order, "z", (2, 1))
    pieces, mine = lax.optimization_barrier((pieces, mine))
    gradient = jnp.sum(pieces.astype(jnp.float32), axis=0)

    squares = jnp.sum(gradient * gradient, axis=0, keepdims=True)
    squares = sum(squares[:, i : i + 128] for i in range(0, cols, 128))
    squares = spread(squares, DP + GROUP, N_ALL)

    weight = order_rows(mine, swap_cores(mine), order, rows)
    grad_input = jnp.einsum(
        "ct,cd->td", cot, weight, preferred_element_type=jnp.float32
    ).astype(jnp.bfloat16)
    squares, grad_input = lax.optimization_barrier((squares, grad_input))

    square_total = jnp.sum(squares)
    factor = jnp.minimum(1.0, CLIP / (jnp.sqrt(square_total) + EPS_NORM))
    clipped = gradient * factor
    new_moment_one = BETA_ONE * moment_one + (1.0 - BETA_ONE) * clipped
    new_moment_two = BETA_TWO * moment_two + (1.0 - BETA_TWO) * clipped * clipped
    first_fix = 1.0 - BETA_ONE**10
    second_fix = 1.0 - BETA_TWO**10
    update = new_moment_one / first_fix / (jnp.sqrt(new_moment_two / second_fix) + EPS_ADAM)
    new_master = master - LEARN_RATE * (update + DECAY_RATE * master)

    return (grad_input, new_master, new_moment_one, new_moment_two)


def solution(mesh):
    fine = Mesh(mesh.devices.reshape(tuple(SIZES.values())), tuple(SIZES))
    return jax.shard_map(
        shards,
        mesh=fine,
        in_specs=(P(DP, GROUP),) * 7,
        out_specs=(P(DP, GROUP),) * 4,
        check_vma=False,
    )
```

```python
import functools

import jax
import jax.numpy as jnp
from jax import lax
from jax.experimental import pallas as pl
from jax.experimental.pallas import tpu as pltpu
from jax.sharding import Mesh
from jax.sharding import PartitionSpec as P


BLOCK = 256
CLIP = 2048


BETA_ONE = 0.9
BETA_TWO = 0.95
LEARN_RATE = 0.25
DECAY_RATE = 0.1
EPS_ADAM = 1e-08
EPS_NORM = 1e-06

SIZES = {"xh": 4, "z": 8, "core": 2, "xl": 2, "y": 8}
DP = ("xh", "z", "core")
GROUP = ("xl", "y")
CHIPS = ("xh", "z")
N_CHIPS = 32
N_GROUP = 16


def dequantize(codes, scales):
    row_count, col_count = codes.shape
    blocked = (
        codes.astype(jnp.float32).reshape(row_count, col_count // BLOCK, BLOCK)
        * scales.astype(jnp.float32)[:, :, None]
    )
    return blocked.reshape(row_count, col_count).astype(jnp.bfloat16)


def spread(block, axes, count):
    return lax.all_to_all(jnp.broadcast_to(block[None], (count, *block.shape)), axes, 0, 0)


def swap_cores(block):
    return lax.ppermute(block, "core", [(0, 1), (1, 0)])


def fetch(block, axis, distance):
    size = SIZES[axis]
    return lax.ppermute(block, axis, [(i, (i - distance) % size) for i in range(size)])


def collect(block, order, axis, distances, share=1):
    part = block[: block.shape[0] // share]
    near = order[: len(order) // share]
    for d in distances:
        step = d % SIZES[axis]
        order = order + [(x + step, z) if axis == "xh" else (x, z + step) for x, z in near]
    return jnp.concatenate([block] + [fetch(part, axis, d) for d in distances], axis=0), order


def order_rows_kernel(order, rows, place_ref, mine_ref, other_ref, out_ref):
    x_own, z_own, core = place_ref[0], place_ref[1], place_ref[2]
    for i, (dx, dz) in enumerate(order):
        chip = lax.rem(x_own + dx, SIZES["xh"]) * SIZES["z"] + lax.rem(z_own + dz, SIZES["z"])
        for source, side in ((mine_ref, core), (other_ref, 1 - core)):
            start = pl.multiple_of((chip * 2 + side) * rows, rows)
            out_ref[pl.ds(start, rows), :] = source[i * rows : (i + 1) * rows, :]


def order_rows(mine, other, order, rows):
    place = jnp.stack([lax.axis_index("xh"), lax.axis_index("z"), lax.axis_index("core")])
    size = 2 * mine.shape[0] * mine.shape[1]
    return pl.pallas_call(
        functools.partial(order_rows_kernel, order, rows),
        out_shape=jax.ShapeDtypeStruct((2 * mine.shape[0], mine.shape[1]), mine.dtype),
        in_specs=[
            pl.BlockSpec(memory_space=pltpu.SMEM),
            pl.BlockSpec(memory_space=pltpu.VMEM),
            pl.BlockSpec(memory_space=pltpu.VMEM),
        ],
        out_specs=pl.BlockSpec(memory_space=pltpu.VMEM),
        cost_estimate=pl.CostEstimate(flops=0, bytes_accessed=4 * size, transcendentals=0),
        compiler_params=pltpu.CompilerParams(vmem_limit_bytes=8 * 2**20),
        name="order_rows",
    )(place.astype(jnp.int32), mine, other)


def work(layer_input, kv_cotangent, weight_codes, block_scales, master, moment_one, moment_two):
    core = lax.axis_index("core")
    rows, cols = weight_codes.shape
    tokens = kv_cotangent.shape[0]

    cot = spread(kv_cotangent.T, GROUP, N_GROUP).reshape(-1, tokens)
    input_other = swap_cores(layer_input)
    mine, order = collect(dequantize(weight_codes, block_scales), [(0, 0)], "xh", (2,))
    mine, order = collect(mine, order, "xh", (1,))
    cot, input_other, mine = lax.optimization_barrier((cot, input_other, mine))

    halves = cot.reshape(N_CHIPS, 2, rows, tokens)
    keep = lax.dynamic_index_in_dim(halves, core, 1, keepdims=False)
    cot_other = swap_cores(lax.dynamic_index_in_dim(halves, 1 - core, 1, keepdims=False))
    pair = jnp.einsum("crt,td->crd", keep, layer_input, preferred_element_type=jnp.float32)
    pair += jnp.einsum("crt,td->crd", cot_other, input_other, preferred_element_type=jnp.float32)
    pieces = lax.all_to_all(pair.astype(jnp.bfloat16), CHIPS, 0, 0)
    mine, order = collect(mine, order, "z", (4,))
    mine, order = collect(mine, order, "z", (2, -2), share=2)
    pieces, mine = lax.optimization_barrier((pieces, mine))
    gradient = jnp.sum(pieces.astype(jnp.float32), axis=0)

    squares = jnp.sum((gradient * gradient).reshape(-1, 8, cols), axis=0)
    squares = sum(squares[:, i : i + 128] for i in range(0, cols, 128))
    squares = spread(squares, CHIPS, N_CHIPS)
    mine, order = collect(mine, order, "z", (1, -1), share=2)
    squares, mine = lax.optimization_barrier((squares, mine))
    squares = spread(jnp.sum(squares, axis=0), ("core",) + GROUP, 2 * N_GROUP)
    weight = order_rows(mine, swap_cores(mine), order, rows)
    grad_input = jnp.einsum(
        "ct,cd->td", cot, weight, preferred_element_type=jnp.float32
    ).astype(jnp.bfloat16)
    squares, grad_input = lax.optimization_barrier((squares, grad_input))
    square_total = jnp.sum(squares)
    factor = jnp.minimum(1.0, CLIP / (jnp.sqrt(square_total) + EPS_NORM))
    clipped = gradient * factor
    new_moment_one = BETA_ONE * moment_one + (1.0 - BETA_ONE) * clipped
    new_moment_two = BETA_TWO * moment_two + (1.0 - BETA_TWO) * clipped * clipped
    first_fix = 1.0 - BETA_ONE**10
    second_fix = 1.0 - BETA_TWO**10
    update = new_moment_one / first_fix / (jnp.sqrt(new_moment_two / second_fix) + EPS_ADAM)
    new_master = master - LEARN_RATE * (update + DECAY_RATE * master)

    return (grad_input, new_master, new_moment_one, new_moment_two)


def solution(mesh):
    fine = Mesh(mesh.devices.reshape(tuple(SIZES.values())), tuple(SIZES))
    return jax.shard_map(
        work,
        mesh=fine,
        in_specs=(P(DP, GROUP),) * 7,
        out_specs=(P(DP, GROUP),) * 4,
        check_vma=False,
    )
```

```python
import functools

import jax
import jax.numpy as jnp
from jax import lax
from jax.experimental import pallas as pl
from jax.experimental.pallas import tpu as pltpu
from jax.sharding import Mesh
from jax.sharding import PartitionSpec as P


BLOCK = 256
CLIP = 2048


BETA_ONE = 0.9
BETA_TWO = 0.95
LEARN_RATE = 0.25
DECAY_RATE = 0.1
EPS_ADAM = 1e-08
EPS_NORM = 1e-06

SIZES = {"xh": 4, "z": 8, "core": 2, "xl": 2, "y": 8}
DP = ("xh", "z", "core")
GROUP = ("xl", "y")
CHIPS = ("xh", "z")
N_CHIPS = 32
N_GROUP = 16


def dequantize(codes, scales):
    row_count, col_count = codes.shape
    blocked = (
        codes.astype(jnp.float32).reshape(row_count, col_count // BLOCK, BLOCK)
        * scales.astype(jnp.float32)[:, :, None]
    )
    return blocked.reshape(row_count, col_count).astype(jnp.bfloat16)


def spread(block, axes, count):
    return lax.all_to_all(jnp.broadcast_to(block[None], (count, *block.shape)), axes, 0, 0)


def swap_cores(block):
    return lax.ppermute(block, "core", [(0, 1), (1, 0)])


def fetch(block, axis, distance):
    size = SIZES[axis]
    return lax.ppermute(block, axis, [(i, (i - distance) % size) for i in range(size)])


def collect(block, order, axis, takes, lead=0):
    rows = block.shape[0] // len(order)
    parts, places = [], []
    for distance, first, last in takes:
        step = distance % SIZES[axis]
        parts.append(fetch(block[first * rows : last * rows], axis, distance))
        places.append([(x + step, z) if axis == "xh" else (x, z + step) for x, z in order[first:last]])
    parts.insert(lead, block)
    places.insert(lead, order)
    return jnp.concatenate(parts, axis=0), sum(places, [])


def order_rows_kernel(order, rows, place_ref, mine_ref, other_ref, out_ref):
    x_own, z_own, core = place_ref[0], place_ref[1], place_ref[2]
    for i, (dx, dz) in enumerate(order):
        chip = lax.rem(x_own + dx, SIZES["xh"]) * SIZES["z"] + lax.rem(z_own + dz, SIZES["z"])
        for source, side in ((mine_ref, core), (other_ref, 1 - core)):
            start = pl.multiple_of((chip * 2 + side) * rows, rows)
            out_ref[pl.ds(start, rows), :] = source[i * rows : (i + 1) * rows, :]


def order_rows(mine, other, order, rows):
    place = jnp.stack([lax.axis_index("xh"), lax.axis_index("z"), lax.axis_index("core")])
    size = 2 * mine.shape[0] * mine.shape[1]
    return pl.pallas_call(
        functools.partial(order_rows_kernel, order, rows),
        out_shape=jax.ShapeDtypeStruct((2 * mine.shape[0], mine.shape[1]), mine.dtype),
        in_specs=[
            pl.BlockSpec(memory_space=pltpu.SMEM),
            pl.BlockSpec(memory_space=pltpu.VMEM),
            pl.BlockSpec(memory_space=pltpu.VMEM),
        ],
        out_specs=pl.BlockSpec(memory_space=pltpu.VMEM),
        cost_estimate=pl.CostEstimate(flops=0, bytes_accessed=4 * size, transcendentals=0),
        compiler_params=pltpu.CompilerParams(vmem_limit_bytes=8 * 2**20),
        name="order_rows",
    )(place.astype(jnp.int32), mine, other)


def work(layer_input, kv_cotangent, weight_codes, block_scales, master, moment_one, moment_two):
    core = lax.axis_index("core")
    rows, cols = weight_codes.shape
    tokens = kv_cotangent.shape[0]

    cot = spread(kv_cotangent.T, GROUP, N_GROUP).reshape(-1, tokens)
    input_other = swap_cores(layer_input)
    mine, order = collect(dequantize(weight_codes, block_scales), [(0, 0)], "xh", ((2, 0, 1),))
    mine, order = collect(mine, order, "xh", ((1, 0, 2),))
    cot, input_other, mine = lax.optimization_barrier((cot, input_other, mine))

    halves = cot.reshape(N_CHIPS, 2, rows, tokens)
    keep = lax.dynamic_index_in_dim(halves, core, 1, keepdims=False)
    cot_other = swap_cores(lax.dynamic_index_in_dim(halves, 1 - core, 1, keepdims=False))
    pair = jnp.einsum("crt,td->crd", keep, layer_input, preferred_element_type=jnp.float32)
    pair += jnp.einsum("crt,td->crd", cot_other, input_other, preferred_element_type=jnp.float32)
    pieces = lax.all_to_all(pair.astype(jnp.bfloat16), CHIPS, 0, 0)
    mine, order = collect(mine, order, "z", ((2, 0, 4), (-2, 0, 4)), lead=1)
    pieces, mine = lax.optimization_barrier((pieces, mine))
    gradient = jnp.sum(pieces.astype(jnp.float32), axis=0)

    squares = jnp.sum((gradient * gradient).reshape(-1, 8, cols), axis=0)
    squares = sum(squares[:, i : i + 128] for i in range(0, cols, 128))
    squares = spread(squares, CHIPS, N_CHIPS)
    mine, order = collect(mine, order, "z", ((1, 0, 8), (-1, 4, 12), (2, 0, 4)))
    squares, mine = lax.optimization_barrier((squares, mine))
    squares = spread(jnp.sum(squares, axis=0), ("core",) + GROUP, 2 * N_GROUP)
    weight = order_rows(mine, swap_cores(mine), order, rows)
    grad_input = jnp.einsum(
        "ct,cd->td", cot, weight, preferred_element_type=jnp.float32
    ).astype(jnp.bfloat16)
    squares, grad_input = lax.optimization_barrier((squares, grad_input))
    square_total = jnp.sum(squares)
    factor = jnp.minimum(1.0, CLIP / (jnp.sqrt(square_total) + EPS_NORM))
    clipped = gradient * factor
    new_moment_one = BETA_ONE * moment_one + (1.0 - BETA_ONE) * clipped
    new_moment_two = BETA_TWO * moment_two + (1.0 - BETA_TWO) * clipped * clipped
    first_fix = 1.0 - BETA_ONE**10
    second_fix = 1.0 - BETA_TWO**10
    update = new_moment_one / first_fix / (jnp.sqrt(new_moment_two / second_fix) + EPS_ADAM)
    new_master = master - LEARN_RATE * (update + DECAY_RATE * master)

    return (grad_input, new_master, new_moment_one, new_moment_two)


def solution(mesh):
    fine = Mesh(mesh.devices.reshape(tuple(SIZES.values())), tuple(SIZES))
    return jax.shard_map(
        work,
        mesh=fine,
        in_specs=(P(DP, GROUP),) * 7,
        out_specs=(P(DP, GROUP),) * 4,
        check_vma=False,
    )
```

```python
import functools

import jax
import jax.numpy as jnp
from jax import lax
from jax.experimental import pallas as pl
from jax.experimental.pallas import tpu as pltpu
from jax.sharding import Mesh
from jax.sharding import PartitionSpec as P


BLOCK = 256
CLIP = 2048


BETA_ONE = 0.9
BETA_TWO = 0.95
LEARN_RATE = 0.25
DECAY_RATE = 0.1
EPS_ADAM = 1e-08
EPS_NORM = 1e-06

SIZES = {"xh": 4, "z": 8, "core": 2, "xl": 2, "y": 8}
DP = ("xh", "z", "core")
GROUP = ("xl", "y")
CHIPS = ("xh", "z")
N_CHIPS = 32
N_GROUP = 16


def dequantize(codes, scales):
    row_count, col_count = codes.shape
    blocked = (
        codes.astype(jnp.float32).reshape(row_count, col_count // BLOCK, BLOCK)
        * scales.astype(jnp.float32)[:, :, None]
    )
    return blocked.reshape(row_count, col_count).astype(jnp.bfloat16)


def spread(block, axes, count):
    return lax.all_to_all(jnp.broadcast_to(block[None], (count, *block.shape)), axes, 0, 0)


def swap_cores(block):
    return lax.ppermute(block, "core", [(0, 1), (1, 0)])


def fetch(block, axis, distance):
    size = SIZES[axis]
    return lax.ppermute(block, axis, [(i, (i - distance) % size) for i in range(size)])


def collect(block, order, axis, takes, lead=0):
    rows = block.shape[0] // len(order)
    parts, places = [], []
    for distance, first, last in takes:
        step = distance % SIZES[axis]
        parts.append(fetch(block[first * rows : last * rows], axis, distance))
        places.append([(x + step, z) if axis == "xh" else (x, z + step) for x, z in order[first:last]])
    parts.insert(lead, block)
    places.insert(lead, order)
    return jnp.concatenate(parts, axis=0), sum(places, [])


def order_rows_kernel(order, rows, place_ref, mine_ref, other_ref, out_ref):
    x_own, z_own, core = place_ref[0], place_ref[1], place_ref[2]
    for i, (dx, dz) in enumerate(order):
        chip = lax.rem(x_own + dx, SIZES["xh"]) * SIZES["z"] + lax.rem(z_own + dz, SIZES["z"])
        for source, side in ((mine_ref, core), (other_ref, 1 - core)):
            start = pl.multiple_of((chip * 2 + side) * rows, rows)
            out_ref[pl.ds(start, rows), :] = source[i * rows : (i + 1) * rows, :]


def order_rows(mine, other, order, rows):
    place = jnp.stack([lax.axis_index("xh"), lax.axis_index("z"), lax.axis_index("core")])
    size = 2 * mine.shape[0] * mine.shape[1]
    return pl.pallas_call(
        functools.partial(order_rows_kernel, order, rows),
        out_shape=jax.ShapeDtypeStruct((2 * mine.shape[0], mine.shape[1]), mine.dtype),
        in_specs=[
            pl.BlockSpec(memory_space=pltpu.SMEM),
            pl.BlockSpec(memory_space=pltpu.VMEM),
            pl.BlockSpec(memory_space=pltpu.VMEM),
        ],
        out_specs=pl.BlockSpec(memory_space=pltpu.VMEM),
        cost_estimate=pl.CostEstimate(flops=0, bytes_accessed=4 * size, transcendentals=0),
        compiler_params=pltpu.CompilerParams(vmem_limit_bytes=8 * 2**20),
        name="order_rows",
    )(place.astype(jnp.int32), mine, other)


def work(layer_input, kv_cotangent, weight_codes, block_scales, master, moment_one, moment_two):
    core = lax.axis_index("core")
    rows, cols = weight_codes.shape
    tokens = kv_cotangent.shape[0]

    cot = spread(kv_cotangent.T, GROUP, N_GROUP).reshape(-1, tokens)
    input_other = swap_cores(layer_input)
    mine, order = collect(
        dequantize(weight_codes, block_scales), [(0, 0)], "xh", ((2, 0, 1), (1, 0, 1), (-1, 0, 1))
    )
    cot, input_other, _ = lax.optimization_barrier((cot, input_other, mine))
    mine, order = collect(mine, order, "z", ((2, 0, 4), (-2, 0, 4)), lead=1)

    halves = cot.reshape(N_CHIPS, 2, rows, tokens)
    keep = lax.dynamic_index_in_dim(halves, core, 1, keepdims=False)
    give = lax.dynamic_index_in_dim(halves, 1 - core, 1, keepdims=False)
    cot_other = swap_cores(give)
    pair = jnp.einsum("crt,td->crd", keep, layer_input, preferred_element_type=jnp.float32)
    pair += jnp.einsum("crt,td->crd", cot_other, input_other, preferred_element_type=jnp.float32)
    pieces = lax.all_to_all(pair.astype(jnp.bfloat16), CHIPS, 0, 0)
    pieces, mine = lax.optimization_barrier((pieces, mine))
    gradient = jnp.sum(pieces.astype(jnp.float32), axis=0)

    squares = jnp.sum((gradient * gradient).reshape(-1, 8, cols), axis=0)
    squares = sum(squares[:, i : i + 128] for i in range(0, cols, 128))
    squares = spread(squares, CHIPS, N_CHIPS)
    mine, order = collect(mine, order, "z", ((1, 0, 8), (-1, 4, 12), (2, 0, 4)))
    squares, mine = lax.optimization_barrier((squares, mine))
    squares = spread(jnp.sum(squares, axis=0), ("core",) + GROUP, 2 * N_GROUP)
    weight = order_rows(mine, swap_cores(mine), order, rows)
    grad_input = jnp.einsum(
        "ct,cd->td", cot, weight, preferred_element_type=jnp.float32
    ).astype(jnp.bfloat16)
    squares, grad_input = lax.optimization_barrier((squares, grad_input))
    square_total = jnp.sum(squares)
    factor = jnp.minimum(1.0, CLIP / (jnp.sqrt(square_total) + EPS_NORM))
    clipped = gradient * factor
    new_moment_one = BETA_ONE * moment_one + (1.0 - BETA_ONE) * clipped
    new_moment_two = BETA_TWO * moment_two + (1.0 - BETA_TWO) * clipped * clipped
    first_fix = 1.0 - BETA_ONE**10
    second_fix = 1.0 - BETA_TWO**10
    update = new_moment_one / first_fix / (jnp.sqrt(new_moment_two / second_fix) + EPS_ADAM)
    new_master = master - LEARN_RATE * (update + DECAY_RATE * master)

    return (grad_input, new_master, new_moment_one, new_moment_two)


def solution(mesh):
    fine = Mesh(mesh.devices.reshape(tuple(SIZES.values())), tuple(SIZES))
    return jax.shard_map(
        work,
        mesh=fine,
        in_specs=(P(DP, GROUP),) * 7,
        out_specs=(P(DP, GROUP),) * 4,
        check_vma=False,
    )
```

```python
import functools

import jax
import jax.numpy as jnp
from jax import lax
from jax.experimental import pallas as pl
from jax.experimental.pallas import tpu as pltpu
from jax.sharding import Mesh
from jax.sharding import PartitionSpec as P


BLOCK = 256
CLIP = 2048


BETA_ONE = 0.9
BETA_TWO = 0.95
LEARN_RATE = 0.25
DECAY_RATE = 0.1
EPS_ADAM = 1e-08
EPS_NORM = 1e-06

SIZES = {"xh": 4, "z": 8, "core": 2, "xl": 2, "y": 8}
DP = ("xh", "z", "core")
GROUP = ("xl", "y")
CHIPS = ("xh", "z")
N_CHIPS = 32
N_GROUP = 16


def dequantize(codes, scales):
    row_count, col_count = codes.shape
    blocked = (
        codes.astype(jnp.float32).reshape(row_count, col_count // BLOCK, BLOCK)
        * scales.astype(jnp.float32)[:, :, None]
    )
    return blocked.reshape(row_count, col_count).astype(jnp.bfloat16)


def spread(block, axes, count):
    return lax.all_to_all(jnp.broadcast_to(block[None], (count, *block.shape)), axes, 0, 0)


def swap_cores(block):
    return lax.ppermute(block, "core", [(0, 1), (1, 0)])


def fetch(block, axis, distance):
    size = SIZES[axis]
    return lax.ppermute(block, axis, [(i, (i - distance) % size) for i in range(size)])


def collect(block, order, axis, takes):
    rows = block.shape[0] // len(order)
    parts, places = [block], list(order)
    for distance, first, last in takes:
        step = distance % SIZES[axis]
        parts.append(fetch(block[first * rows : last * rows], axis, distance))
        places += [(x + step, z) if axis == "xh" else (x, z + step) for x, z in order[first:last]]
    return lax.optimization_barrier(jnp.concatenate(parts, axis=0)), places


def order_rows_kernel(order, rows, place_ref, mine_ref, other_ref, out_ref):
    x_own, z_own, core = place_ref[0], place_ref[1], place_ref[2]
    for i, (dx, dz) in enumerate(order):
        chip = lax.rem(x_own + dx, SIZES["xh"]) * SIZES["z"] + lax.rem(z_own + dz, SIZES["z"])
        for source, side in ((mine_ref, core), (other_ref, 1 - core)):
            start = pl.multiple_of((chip * 2 + side) * rows, rows)
            out_ref[pl.ds(start, rows), :] = source[i * rows : (i + 1) * rows, :]


def order_rows(mine, other, order, rows):
    place = jnp.stack([lax.axis_index("xh"), lax.axis_index("z"), lax.axis_index("core")])
    size = 2 * mine.shape[0] * mine.shape[1]
    return pl.pallas_call(
        functools.partial(order_rows_kernel, order, rows),
        out_shape=jax.ShapeDtypeStruct((2 * mine.shape[0], mine.shape[1]), mine.dtype),
        in_specs=[
            pl.BlockSpec(memory_space=pltpu.SMEM),
            pl.BlockSpec(memory_space=pltpu.VMEM),
            pl.BlockSpec(memory_space=pltpu.VMEM),
        ],
        out_specs=pl.BlockSpec(memory_space=pltpu.VMEM),
        cost_estimate=pl.CostEstimate(flops=0, bytes_accessed=4 * size, transcendentals=0),
        compiler_params=pltpu.CompilerParams(vmem_limit_bytes=8 * 2**20),
        name="order_rows",
    )(place.astype(jnp.int32), mine, other)


def work(layer_input, kv_cotangent, weight_codes, block_scales, master, moment_one, moment_two):
    core = lax.axis_index("core")
    rows, cols = weight_codes.shape
    tokens = kv_cotangent.shape[0]

    cot = spread(kv_cotangent.T, GROUP, N_GROUP).reshape(-1, tokens)
    input_other = swap_cores(layer_input)
    mine, order = collect(
        dequantize(weight_codes, block_scales), [(0, 0)], "xh", ((2, 0, 1), (1, 0, 1), (-1, 0, 1))
    )
    cot, input_other, _ = lax.optimization_barrier((cot, input_other, mine))
    mine, order = collect(mine, order, "z", ((3, 0, 4), (-3, 0, 4)))

    halves = cot.reshape(N_CHIPS, 2, rows, tokens)
    keep = lax.dynamic_index_in_dim(halves, core, 1, keepdims=False)
    give = lax.dynamic_index_in_dim(halves, 1 - core, 1, keepdims=False)
    cot_other = swap_cores(give)
    pair = jnp.einsum("crt,td->crd", keep, layer_input, preferred_element_type=jnp.float32)
    pair += jnp.einsum("crt,td->crd", cot_other, input_other, preferred_element_type=jnp.float32)
    pieces = lax.all_to_all(pair.astype(jnp.bfloat16), CHIPS, 0, 0)
    pieces, mine = lax.optimization_barrier((pieces, mine))
    gradient = jnp.sum(pieces.astype(jnp.float32), axis=0)

    squares = jnp.sum((gradient * gradient).reshape(-1, 8, cols), axis=0)
    squares = sum(squares[:, i : i + 128] for i in range(0, cols, 128))
    squares = spread(squares, CHIPS, N_CHIPS)
    mine, order = collect(mine, order, "z", ((1, 0, 12), (-1, 0, 8)))
    squares, mine = lax.optimization_barrier((squares, mine))
    squares = spread(jnp.sum(squares, axis=0), ("core",) + GROUP, 2 * N_GROUP)
    weight = order_rows(mine, swap_cores(mine), order, rows)
    grad_input = jnp.einsum(
        "ct,cd->td", cot, weight, preferred_element_type=jnp.float32
    ).astype(jnp.bfloat16)
    squares, grad_input = lax.optimization_barrier((squares, grad_input))
    square_total = jnp.sum(squares)
    factor = jnp.minimum(1.0, CLIP / (jnp.sqrt(square_total) + EPS_NORM))
    clipped = gradient * factor
    new_moment_one = BETA_ONE * moment_one + (1.0 - BETA_ONE) * clipped
    new_moment_two = BETA_TWO * moment_two + (1.0 - BETA_TWO) * clipped * clipped
    first_fix = 1.0 - BETA_ONE**10
    second_fix = 1.0 - BETA_TWO**10
    update = new_moment_one / first_fix / (jnp.sqrt(new_moment_two / second_fix) + EPS_ADAM)
    new_master = master - LEARN_RATE * (update + DECAY_RATE * master)

    return (grad_input, new_master, new_moment_one, new_moment_two)


def solution(mesh):
    fine = Mesh(mesh.devices.reshape(tuple(SIZES.values())), tuple(SIZES))
    return jax.shard_map(
        work,
        mesh=fine,
        in_specs=(P(DP, GROUP),) * 7,
        out_specs=(P(DP, GROUP),) * 4,
        check_vma=False,
    )
```

```python
import functools

import jax
import jax.numpy as jnp
from jax import lax
from jax.experimental import pallas as pl
from jax.experimental.pallas import tpu as pltpu
from jax.sharding import Mesh
from jax.sharding import PartitionSpec as P


BLOCK = 256
CLIP = 2048


BETA_ONE = 0.9
BETA_TWO = 0.95
LEARN_RATE = 0.25
DECAY_RATE = 0.1
EPS_ADAM = 1e-08
EPS_NORM = 1e-06

SIZES = {"xh": 4, "z": 8, "core": 2, "xl": 2, "y": 8}
DP = ("xh", "z", "core")
GROUP = ("xl", "y")
CHIPS = ("xh", "z")
N_CHIPS = 32
N_GROUP = 16


def dequantize(codes, scales):
    row_count, col_count = codes.shape
    blocked = (
        codes.astype(jnp.float32).reshape(row_count, col_count // BLOCK, BLOCK)
        * scales.astype(jnp.float32)[:, :, None]
    )
    return blocked.reshape(row_count, col_count).astype(jnp.bfloat16)


def spread(block, axes, count):
    return lax.all_to_all(jnp.broadcast_to(block[None], (count, *block.shape)), axes, 0, 0)


def copies_kernel(count, block_ref, out_ref):
    turned = block_ref[...].T
    for i in range(count):
        out_ref[i] = turned


def copies_turned(block, count):
    rows, cols = block.shape
    return pl.pallas_call(
        functools.partial(copies_kernel, count),
        out_shape=jax.ShapeDtypeStruct((count, cols, rows), block.dtype),
        in_specs=[pl.BlockSpec(memory_space=pltpu.VMEM)],
        out_specs=pl.BlockSpec(memory_space=pltpu.VMEM),
        cost_estimate=pl.CostEstimate(
            flops=0, bytes_accessed=2 * (count + 1) * rows * cols, transcendentals=0
        ),
        compiler_params=pltpu.CompilerParams(vmem_limit_bytes=4 * 2**20),
        name="copies_turned",
    )(block)


def swap_cores(block):
    return lax.ppermute(block, "core", [(0, 1), (1, 0)])


def fetch(block, axis, distance):
    size = SIZES[axis]
    return lax.ppermute(block, axis, [(i, (i - distance) % size) for i in range(size)])


def collect(block, order, axis, takes):
    rows = block.shape[0] // len(order)
    parts, places = [block], list(order)
    for distance, first, last in takes:
        step = distance % SIZES[axis]
        parts.append(fetch(block[first * rows : last * rows], axis, distance))
        places += [(x + step, z) if axis == "xh" else (x, z + step) for x, z in order[first:last]]
    return lax.optimization_barrier(jnp.concatenate(parts, axis=0)), places


def order_rows_kernel(order, rows, place_ref, mine_ref, other_ref, out_ref):
    x_own, z_own, core = place_ref[0], place_ref[1], place_ref[2]
    for i, (dx, dz) in enumerate(order):
        chip = lax.rem(x_own + dx, SIZES["xh"]) * SIZES["z"] + lax.rem(z_own + dz, SIZES["z"])
        for source, side in ((mine_ref, core), (other_ref, 1 - core)):
            start = pl.multiple_of((chip * 2 + side) * rows, rows)
            out_ref[pl.ds(start, rows), :] = source[i * rows : (i + 1) * rows, :]


def order_rows(mine, other, order, rows):
    place = jnp.stack([lax.axis_index("xh"), lax.axis_index("z"), lax.axis_index("core")])
    size = 2 * mine.shape[0] * mine.shape[1]
    return pl.pallas_call(
        functools.partial(order_rows_kernel, order, rows),
        out_shape=jax.ShapeDtypeStruct((2 * mine.shape[0], mine.shape[1]), mine.dtype),
        in_specs=[
            pl.BlockSpec(memory_space=pltpu.SMEM),
            pl.BlockSpec(memory_space=pltpu.VMEM),
            pl.BlockSpec(memory_space=pltpu.VMEM),
        ],
        out_specs=pl.BlockSpec(memory_space=pltpu.VMEM),
        cost_estimate=pl.CostEstimate(flops=0, bytes_accessed=4 * size, transcendentals=0),
        compiler_params=pltpu.CompilerParams(vmem_limit_bytes=8 * 2**20),
        name="order_rows",
    )(place.astype(jnp.int32), mine, other)


def work(layer_input, kv_cotangent, weight_codes, block_scales, master, moment_one, moment_two):
    core = lax.axis_index("core")
    rows, cols = weight_codes.shape
    tokens = kv_cotangent.shape[0]

    cot = lax.all_to_all(copies_turned(kv_cotangent, N_GROUP), GROUP, 0, 0).reshape(-1, tokens)
    mine, order = collect(
        dequantize(weight_codes, block_scales), [(0, 0)], "xh", ((2, 0, 1), (1, 0, 1), (-1, 0, 1))
    )
    cot, _ = lax.optimization_barrier((cot, mine))
    mine, order = collect(mine, order, "z", ((3, 0, 4), (-3, 0, 4)))

    halves = cot.reshape(N_CHIPS, 2, rows, tokens)
    keep = lax.dynamic_index_in_dim(halves, core, 1, keepdims=False)
    give = lax.dynamic_index_in_dim(halves, 1 - core, 1, keepdims=False)
    cot_other = swap_cores(give)
    input_other = swap_cores(layer_input)
    pair = jnp.einsum("crt,td->crd", keep, layer_input, preferred_element_type=jnp.float32)
    pair += jnp.einsum("crt,td->crd", cot_other, input_other, preferred_element_type=jnp.float32)
    pieces = lax.all_to_all(pair.astype(jnp.bfloat16), CHIPS, 0, 0)
    pieces, mine = lax.optimization_barrier((pieces, mine))
    gradient = jnp.sum(pieces.astype(jnp.float32), axis=0)

    squares = jnp.sum((gradient * gradient).reshape(-1, 8, cols), axis=0)
    squares = sum(squares[:, i : i + 128] for i in range(0, cols, 128))
    squares = spread(squares, CHIPS, N_CHIPS)
    mine, order = collect(mine, order, "z", ((1, 0, 12), (-1, 0, 8)))
    squares = spread(jnp.sum(squares, axis=0), ("core",) + GROUP, 2 * N_GROUP)
    weight = order_rows(mine, swap_cores(mine), order, rows)
    grad_input = jnp.einsum(
        "ct,cd->td", cot, weight, preferred_element_type=jnp.float32
    ).astype(jnp.bfloat16)
    squares, grad_input = lax.optimization_barrier((squares, grad_input))
    square_total = jnp.sum(squares)
    factor = jnp.minimum(1.0, CLIP / (jnp.sqrt(square_total) + EPS_NORM))
    clipped = gradient * factor
    new_moment_one = BETA_ONE * moment_one + (1.0 - BETA_ONE) * clipped
    new_moment_two = BETA_TWO * moment_two + (1.0 - BETA_TWO) * clipped * clipped
    first_fix = 1.0 - BETA_ONE**10
    second_fix = 1.0 - BETA_TWO**10
    update = new_moment_one / first_fix / (jnp.sqrt(new_moment_two / second_fix) + EPS_ADAM)
    new_master = master - LEARN_RATE * (update + DECAY_RATE * master)

    return (grad_input, new_master, new_moment_one, new_moment_two)


def solution(mesh):
    fine = Mesh(mesh.devices.reshape(tuple(SIZES.values())), tuple(SIZES))
    return jax.shard_map(
        work,
        mesh=fine,
        in_specs=(P(DP, GROUP),) * 7,
        out_specs=(P(DP, GROUP),) * 4,
        check_vma=False,
    )
```
